32 devices in a mesh: depth: 4 (over y, x), tile: 8 (over z, core).
Axes of the slice: x: 2, y: 2, z: 4, core: 2. Of those that a mesh axis runs over, the one named last changes fastest.
Arguments:
- density: bfloat16 [128, 512, 2048], P('depth', 'tile'), may hold values from 0 to 2
- depth_rank: int32 [4], replicated, may hold values from 0 to 3, as said below
- piece_home: int32 [64], P('tile'), may hold values from 0 to 63, as said below
Outputs:
- display: float32 [3, 4, 64, 4096], P(None, 'depth', 'tile')
The draws below stay inside these ranges and needn't reach their ends.
Inputs may be any that keep to these rules, and one draw needn't show every extreme that they name: Either depth_rank[i] = i for every i, or depth_rank[i] = 3 - i for every i. `piece_home`: every value appears exactly once. A value h names slot h % 8 of the device h // 8 along tile. The number of the 8 entries of tile device s that name device o depends only on (o - s) mod 8, is at most 2, and equals 2 for some pair.
All inputs are finite; a program needn't handle non-finite values.
Results may differ from the reference program's by a relative error of at most 0.0003.
Values may be sent and summed in bfloat16 or wider, within the bound.
A program may use at most 128 MiB of HBM per device.

```python
import math
from functools import partial
import jax
import jax.numpy as jnp
from jax import lax

CZ = 32
BY = 64
IMAGE_COLUMNS = 2048
VIEW_CELLS = 128
IMAGE_ROWS = 512
PPD = 8
PR = 4096
PIECES = 64
N_DEPTH = 4
N_TILE = 8


def draw_density(key, part):
    random_keys = jax.random.split(key, 4)
    low_end, high_end = (0.003, 0.25)
    logs = jax.random.uniform(random_keys[0], (1, IMAGE_ROWS, IMAGE_COLUMNS), jnp.float32, math.log(low_end), math.log(high_end))
    column_weighting = jnp.exp(logs)
    surface_bumpiness = jax.random.uniform(random_keys[1], (VIEW_CELLS, IMAGE_ROWS, IMAGE_COLUMNS), jnp.float32, 0.5, 1.5)
    spike_row_indices = jax.random.randint(random_keys[2], (3,), 0, VIEW_CELLS)
    slice_depth_index = jnp.arange(VIEW_CELLS)
    spike_active = jnp.any(slice_depth_index[:, None] == spike_row_indices[None, :], axis=1).astype(jnp.float32)
    spike_multiplier = jax.random.uniform(random_keys[3], (1, IMAGE_ROWS, IMAGE_COLUMNS), jnp.float32, 0.5, 1.5)
    solute_field_value = column_weighting * surface_bumpiness + 0.7 * spike_active[:, None, None] * spike_multiplier
    return solute_field_value.astype(jnp.bfloat16)


def draw_depth_rank(key, part):
    brick_count = VIEW_CELLS // CZ
    flipped = jax.random.randint(key, (), 0, 2)
    positions = jnp.arange(brick_count)
    return jnp.where(flipped == 1, brick_count - 1 - positions, positions).astype(jnp.int32)


def draw_piece_home(key, part):
    tile_count = IMAGE_ROWS // BY
    random_keys = jax.random.split(key, 4)
    doubles = jax.random.randint(random_keys[0], (), 1, tile_count // 2 + 1)
    shuffle = jax.random.permutation(random_keys[1], tile_count)
    counts = jnp.where(shuffle < doubles, 2, jnp.where(shuffle < 2 * doubles, 0, 1)).astype(jnp.int32)
    bounds = jnp.cumsum(counts)
    permuter = jax.vmap(partial(jax.random.permutation, x=PPD))
    ranks = permuter(jax.random.split(random_keys[2], tile_count)).astype(jnp.int32)
    offsets = jnp.sum((bounds[None, None, :] <= ranks[:, :, None]).astype(jnp.int32), axis=2)
    owners = (jnp.arange(tile_count, dtype=jnp.int32)[:, None] + offsets) % tile_count
    slots = permuter(jax.random.split(random_keys[3], tile_count)).astype(jnp.int32)
    homes = owners * PPD + slots[owners, ranks]
    return homes.reshape(-1).astype(jnp.int32)


def setup_inputs(seed: int = 0) -> dict:
    arg_keys = jax.random.split(jax.random.key(seed), 4)
    density = draw_density(jax.random.fold_in(arg_keys[3], 71), 0)
    depth_rank = draw_depth_rank(jax.random.fold_in(arg_keys[3], 71), 0)
    piece_home = draw_piece_home(jax.random.fold_in(arg_keys[3], 71), 0)
    return {"density": density, "depth_rank": depth_rank, "piece_home": piece_home}


EXTINCT = 0.5
LIGHT_Z = 0.6
LIGHT_Y = 0.48
LIGHT_X = 0.64
SHARPNESS = 6.0
BACKDROP = (0.08, 0.1, 0.14)


def lighting(padded):
    center = padded[1:-1, 1:-1, :]
    grad_z = 0.5 * (padded[2:, 1:-1, :] - padded[:-2, 1:-1, :])
    grad_y = 0.5 * (padded[1:-1, 2:, :] - padded[1:-1, :-2, :])
    padded_x = jnp.pad(center, ((0, 0), (0, 0), (1, 1)))
    grad_x = 0.5 * (padded_x[:, :, 2:] - padded_x[:, :, :-2])
    facing = LIGHT_Z * grad_z + LIGHT_Y * grad_y + LIGHT_X * grad_x
    shading = 0.35 + 0.65 * (0.5 + 0.5 * jnp.tanh(SHARPNESS * facing))
    return center, shading


def emission(center):
    logged = jnp.log(center + 0.01)
    return (jax.nn.sigmoid(logged + 3.0), 0.5 + 0.5 * jnp.cos(1.7 * logged), jax.nn.sigmoid(-(logged + 2.5)))


def reference(density, depth_rank, piece_home):
    ascend = depth_rank[0] == 0
    padded = jnp.pad(density, ((1, 1), (1, 1), (0, 0)))
    backdrop = jnp.array(BACKDROP, jnp.float32)[:, None, None]

    def one_block(block_index):
        first_row = (block_index * BY).astype(jnp.int32)
        window = lax.dynamic_slice_in_dim(padded, first_row, BY + 2, 1).astype(jnp.float32)
        center, shading = lighting(window)
        optical = EXTINCT * center
        forward = lax.cumsum(optical, 0) - optical
        backward = lax.cumsum(optical, 0, reverse=True) - optical
        before = jnp.where(ascend, forward, backward)
        weight = jnp.exp(-before) * (-jnp.expm1(-optical)) * shading
        colors = emission(center)
        radiance = jnp.stack([jnp.sum(weight * channel, axis=0) for channel in colors])
        through = jnp.exp(-jnp.sum(optical, axis=0))
        return radiance + through[None] * backdrop

    finals = lax.map(one_block, jnp.arange(N_TILE, dtype=jnp.int32))
    pieces = finals.reshape(N_TILE, 3, N_DEPTH, PPD, PR)
    pieces = pieces.transpose(1, 2, 0, 3, 4).reshape(3, N_DEPTH, PIECES, PR)
    display = jnp.zeros_like(pieces).at[:, :, piece_home, :].set(pieces)
    return display
```

```python
import functools
import math
import jax
import jax.numpy as jnp
import numpy as np
from jax import lax
from jax.experimental import pallas as pl
from jax.experimental.pallas import tpu as pltpu
from jax.sharding import PartitionSpec as P

MOST = 2

EXTINCT = 0.5
LIGHT_Z = 0.6
LIGHT_Y = 0.48
LIGHT_X = 0.64
SHARPNESS = 6.0
BACKDROP = (0.08, 0.1, 0.14)

HALO = 16
PAD = 128
CB = 256
RB = 16
SIG_A = math.exp(-3.0)
SIG_B = math.exp(-2.5)
COS = (1.9999999935320312, -0.9999997751464547, 0.08333208188264607,
       -0.002775337047259153, 4.7654375196060637e-05)


def stencils(rows):
    span = rows + HALO
    wy, wz = LIGHT_Y / LIGHT_X, LIGHT_Z / LIGHT_X
    left = np.zeros((rows, 3 * span), np.float32)
    for r in range(rows):
        left[r, r] = -wz
        left[r, 2 * span + r] = wz
        left[r, span + (r + 1 if r < rows - 1 else rows)] = wy
        left[r, span + (r - 1 if r > 0 else rows + 1)] = -wy
    right = np.zeros((CB + 2 * PAD, CB), np.float32)
    for c in range(CB):
        right[c + PAD + 1, c] = 1.0
        right[c + PAD - 1, c] = -1.0
    return jnp.asarray(left, jnp.bfloat16), jnp.asarray(right, jnp.bfloat16)


def make_facing(d, g, left, right, cells, rows, zc):
    span = rows + HALO

    def facing(block, slot, chunk):
        z0 = chunk * zc
        c0 = pl.multiple_of(block * CB, CB)
        wide = d[pl.ds(z0 + 1, zc), :, pl.ds(c0, CB + 2 * PAD)]
        dx = jnp.dot(wide.reshape(zc * span, CB + 2 * PAD), right[...],
                     preferred_element_type=jnp.float32)
        c1 = pl.multiple_of(block * CB + PAD, PAD)
        for i in range(zc):
            tall = d[pl.ds(z0 + i, 3), :, pl.ds(c1, CB)].reshape(3 * span, CB)
            dyz = jnp.dot(left[...], tall, preferred_element_type=jnp.float32)
            g[slot, z0 + i] = dyz + dx[i * span:i * span + rows]

    return facing


def march(d, g, state, ascend, block, slot, rb, half, halves, cells):
    steps = cells // halves
    first = half == 0
    shape = (RB, CB)
    trans = jnp.where(first, 1.0, state[0])
    total, m0, m1, wave = (jnp.where(first, 0.0, state[i]) for i in range(1, 5))
    r0 = pl.multiple_of(rb * RB, RB)
    c1 = pl.multiple_of(block * CB + PAD, PAD)
    bias = (0.35 + 0.65 * 0.5) / (0.65 * 0.5)
    for i in range(steps):
        k = half * steps + i
        z = jnp.where(ascend, k, cells - 1 - k)
        dens = d[z + 1, pl.ds(r0, RB), pl.ds(c1, CB)].astype(jnp.float32)
        face = g[slot, z, pl.ds(r0, RB), :]
        shade = jnp.tanh(face * (0.5 * SHARPNESS * LIGHT_X)) + bias
        after = trans * jnp.exp2(dens * (-EXTINCT * math.log2(math.e)))
        ws = (trans - after) * shade
        trans = after
        u = dens + 0.01
        wr = ws / ((u + SIG_A) * (u + SIG_B))
        x = jnp.log(u) * (1.7 / 4) + math.pi / 4
        s = x * x
        c = COS[4] * s + COS[3]
        c = c * s + COS[2]
        c = c * s + COS[1]
        c = c * s + COS[0]
        v = c * c - 2.0
        total = total + ws
        m0 = m0 + wr
        m1 = m1 + wr * u
        wave = wave + ws * (v * v)
    for i, val in enumerate((trans, total, m0, m1, wave)):
        state[i] = val
    scale = 0.65 * 0.5
    return (
        scale * (total - SIG_A * (m1 + SIG_B * m0)),
        scale * (total - 0.25 * wave),
        scale * SIG_B * (m1 + SIG_A * m0),
        trans,
    )


def brick_kernel(rank, dens, zlo, zhi, yh, left, right, out, d, g, state, sems):
    cells, rows, cols = dens.shape
    nb, bands, halves = cols // CB, rows // RB, 2
    its = bands * halves
    zc = cells // its
    ascend = rank[0] == 0

    def copies(block):
        src = pl.ds(pl.multiple_of(block * CB, CB), CB)
        dst = pl.ds(pl.multiple_of(block * CB + PAD, PAD), CB)
        mk = pltpu.make_async_copy
        return (
            mk(dens.at[:, :, src], d.at[pl.ds(1, cells), pl.ds(0, rows), dst], sems.at[0, block]),
            mk(yh.at[:, :, src], d.at[pl.ds(1, cells), pl.ds(rows, HALO), dst], sems.at[1, block]),
            mk(zlo.at[:, src], d.at[0, pl.ds(0, rows), dst], sems.at[2, block]),
            mk(zhi.at[:, src], d.at[cells + 1, pl.ds(0, rows), dst], sems.at[3, block]),
        )

    @pl.loop(0, nb)
    def _(b):
        for cp in copies(b):
            cp.start()

    side = jnp.zeros((cells + 2, rows + HALO, PAD), d.dtype)
    d[:, :, :PAD] = side
    d[:, :, cols + PAD:] = side
    edge = jnp.zeros((HALO, cols), d.dtype)
    d[0, rows:, PAD:cols + PAD] = edge
    d[cells + 1, rows:, PAD:cols + PAD] = edge
    facing = make_facing(d, g, left, right, cells, rows, zc)

    def arrive(b):
        for cp in copies(b):
            cp.wait()

    arrive(0)
    arrive(1)

    @pl.loop(0, its)
    def _(it):
        facing(0, 0, it)

    @pl.loop(0, nb)
    def _(b):
        @pl.when(b + 2 < nb)
        def _():
            arrive(b + 2)

        slot = lax.rem(b, 2)
        ahead = jnp.minimum(b + 1, nb - 1)

        @pl.loop(0, its)
        def _(it):
            facing(ahead, 1 - slot, it)
            rb = it // halves
            vals = march(d, g, state, ascend, b, slot, rb, lax.rem(it, halves), halves, cells)
            for ch, val in enumerate(vals):
                out[ch, pl.ds(pl.multiple_of(rb * RB, RB), RB), pl.ds(pl.multiple_of(b * CB, CB), CB)] = val


def partial_image_of(density, depth_rank, zlo, zhi, yh):
    cells, rows, cols = density.shape
    left, right = stencils(rows)
    anyspec = pl.BlockSpec(memory_space=pl.ANY)
    vmem = pl.BlockSpec(memory_space=pltpu.VMEM)
    return pl.pallas_call(
        brick_kernel,
        out_shape=jax.ShapeDtypeStruct((4, rows, cols), jnp.float32),
        in_specs=[pl.BlockSpec(memory_space=pltpu.SMEM)] + [anyspec] * 4 + [vmem] * 2,
        out_specs=vmem,
        scratch_shapes=[
            pltpu.VMEM((cells + 2, rows + HALO, cols + 2 * PAD), jnp.bfloat16),
            pltpu.VMEM((2, cells, rows, CB), jnp.float32),
            pltpu.VMEM((5, RB, CB), jnp.float32),
            pltpu.SemaphoreType.DMA((4, cols // CB)),
        ],
        compiler_params=pltpu.CompilerParams(vmem_limit_bytes=48 * 1024 * 1024),
    )(depth_rank, density, zlo, zhi, yh, left, right)


def edges(density):
    cells, rows, cols = density.shape

    def move(x, axis, step):
        n = lax.axis_size(axis)
        return lax.ppermute(x, axis, [(i, i + step) for i in range(n) if 0 <= i + step < n])

    zlo = move(density[cells - 1], "depth", 1)
    zhi = move(density[0], "depth", -1)
    ylo = move(density[:, rows - 1], "tile", 1)
    yhi = move(density[:, 0], "tile", -1)
    yh = jnp.concatenate(
        [yhi[:, None], ylo[:, None], jnp.zeros((cells, HALO - 2, cols), density.dtype)], axis=1
    )
    return zlo, zhi, yh


def on_device(density, depth_rank, piece_home):
    depth_cells, row_count, columns = density.shape
    ascend = depth_rank[0] == 0
    partial_image = partial_image_of(density, depth_rank, *edges(density))
    depth_count = lax.axis_size("depth")
    quarter = row_count * columns // depth_count
    layered = partial_image.reshape(4, depth_count, row_count // depth_count, columns)
    gathered = lax.all_to_all(layered, "depth", split_axis=1, concat_axis=1, tiled=True)
    color_acc = gathered[:3, 0]
    trans_acc = gathered[3:4, 0]
    for member in range(1, depth_count):
        color_new = gathered[:3, member]
        trans_new = gathered[3:4, member]
        color_acc = jnp.where(
            ascend, color_acc + trans_acc * color_new, color_new + trans_new * color_acc
        )
        trans_acc = trans_acc * trans_new
    merged = jnp.concatenate([color_acc, trans_acc], 0)
    backdrop = jnp.array(BACKDROP, jnp.float32)[:, None]
    merged = merged.reshape(4, quarter)
    finished = merged[:3] + merged[3:4] * backdrop
    tile_count = lax.axis_size("tile")
    piece_len = quarter // tile_count
    pieces = finished.reshape(3, tile_count, piece_len)
    owners = piece_home // tile_count
    slots = piece_home % tile_count
    order_index = jnp.arange(tile_count)
    shared = owners[:, None] == owners[None, :]
    earlier_count = jnp.sum(
        (shared & (order_index[None, :] < order_index[:, None])).astype(jnp.int32), axis=1
    )
    target = owners * MOST + earlier_count
    outbox_index = jnp.arange(tile_count * MOST)
    routing = (outbox_index[:, None] == target[None, :]).astype(jnp.float32)
    outbox = jnp.einsum("sp,cpr->scr", routing, pieces, precision=lax.Precision.HIGHEST)
    labels = (
        jnp.dot(routing, (slots + 1).astype(jnp.float32), precision=lax.Precision.HIGHEST) - 1.0
    )
    outbox = outbox.reshape(tile_count, MOST, 3, piece_len)
    labels = labels.reshape(tile_count, MOST)
    arrived, arrived_labels = (
        lax.all_to_all(outbox, "tile", split_axis=0, concat_axis=0, tiled=True),
        lax.all_to_all(labels, "tile", split_axis=0, concat_axis=0, tiled=True),
    )
    flat_pieces = arrived.reshape(tile_count * MOST, 3, piece_len)
    flat_labels = arrived_labels.reshape(-1).astype(jnp.int32)
    placing = (order_index[:, None] == flat_labels[None, :]).astype(jnp.float32)
    display = jnp.einsum("qs,scr->cqr", placing, flat_pieces, precision=lax.Precision.HIGHEST)
    return display[:, None]


def solution(mesh):
    in_specs = (P("depth", "tile", None), P(), P("tile"))
    out_specs = P(None, "depth", "tile", None)
    return jax.shard_map(
        on_device, mesh=mesh, in_specs=in_specs, out_specs=out_specs, check_vma=False
    )
```

```python
import math
import jax
import jax.numpy as jnp
import numpy as np
from jax import lax
from jax.experimental import pallas as pl
from jax.experimental.pallas import tpu as pltpu
from jax.sharding import PartitionSpec as P

MOST = 2

EXTINCT = 0.5
LIGHT_Z = 0.6
LIGHT_Y = 0.48
LIGHT_X = 0.64
SHARPNESS = 6.0
BACKDROP = (0.08, 0.1, 0.14)

PAD = 128
CB = 256
RB = 16
SIG_A = math.exp(-3.0)
SIG_B = math.exp(-2.5)
COS = (1.9999999935320312, -0.9999997751464547, 0.08333208188264607,
       -0.002775337047259153, 4.7654375196060637e-05)


def stencils(rows):
    wy, wz = LIGHT_Y / LIGHT_X, LIGHT_Z / LIGHT_X
    left = np.zeros((rows, 3 * rows), np.float32)
    for r in range(rows):
        left[r, r] = -wz
        left[r, 2 * rows + r] = wz
        if r < rows - 1:
            left[r, rows + r + 1] = wy
        if r > 0:
            left[r, rows + r - 1] = -wy
    right = np.zeros((CB + 2 * PAD, CB), np.float32)
    for c in range(CB):
        right[c + PAD + 1, c] = 1.0
        right[c + PAD - 1, c] = -1.0
    return jnp.asarray(left, jnp.bfloat16), jnp.asarray(right, jnp.bfloat16)


def make_facing(d, g, dens32, hs, left, right, cells, rows, zc):
    wy = LIGHT_Y / LIGHT_X

    def facing(block, slot, chunk):
        z0 = chunk * zc
        c0 = pl.multiple_of(block * CB, CB)
        wide = d[pl.ds(z0 + 1, zc), :, pl.ds(c0, CB + 2 * PAD)]
        dx = jnp.dot(wide.reshape(zc * rows, CB + 2 * PAD), right[...],
                     preferred_element_type=jnp.float32)
        c1 = pl.multiple_of(block * CB + PAD, PAD)
        sub = lax.broadcasted_iota(jnp.int32, (8, CB), 0)
        for i in range(zc):
            tall = d[pl.ds(z0 + i, 3), :, pl.ds(c1, CB)].reshape(3 * rows, CB)
            dyz = jnp.dot(left[...], tall, preferred_element_type=jnp.float32)
            both = dyz + dx[i * rows:(i + 1) * rows]
            low = hs[0, pl.ds(z0 + i, 1), :] * wy
            high = hs[1, pl.ds(z0 + i, 1), :] * wy
            g[slot, z0 + i, 0:8] = both[0:8] - jnp.where(sub == 0, low, 0.0)
            g[slot, z0 + i, 8:rows - 8] = both[8:rows - 8]
            g[slot, z0 + i, rows - 8:rows] = both[rows - 8:] + jnp.where(sub == 7, high, 0.0)
            dens32[slot, z0 + i] = wide[i, :, PAD:PAD + CB].astype(jnp.float32)

    return facing


def march(dens32, g, state, ascend, slot, rb, half, halves, cells):
    steps = cells // halves
    first = half == 0
    trans = jnp.where(first, 1.0, state[0])
    total, m0, m1, wave = (jnp.where(first, 0.0, state[i]) for i in range(1, 5))
    r0 = pl.multiple_of(rb * RB, RB)
    bias = (0.35 + 0.65 * 0.5) / (0.65 * 0.5)
    for i in range(steps):
        k = half * steps + i
        z = jnp.where(ascend, k, cells - 1 - k)
        dens = dens32[slot, z, pl.ds(r0, RB), :]
        face = g[slot, z, pl.ds(r0, RB), :]
        shade = jnp.tanh(face * (0.5 * SHARPNESS * LIGHT_X)) + bias
        after = trans * jnp.exp2(dens * (-EXTINCT * math.log2(math.e)))
        ws = (trans - after) * shade
        trans = after
        u = dens + 0.01
        wr = ws / ((u + SIG_A) * (u + SIG_B))
        x = jnp.log(u) * (1.7 / 4) + math.pi / 4
        s = x * x
        c = COS[4] * s + COS[3]
        c = c * s + COS[2]
        c = c * s + COS[1]
        c = c * s + COS[0]
        v = c * c - 2.0
        total = total + ws
        m0 = m0 + wr
        m1 = m1 + wr * u
        wave = wave + ws * (v * v)
    for i, val in enumerate((trans, total, m0, m1, wave)):
        state[i] = val
    scale = 0.65 * 0.5
    return (
        scale * (total - SIG_A * (m1 + SIG_B * m0)),
        scale * (total - 0.25 * wave),
        scale * SIG_B * (m1 + SIG_A * m0),
        trans,
    )


def brick_kernel(nd, nt, rank, route, dens, ysend, labels, left, right, inbox, arrived,
                 d, hb, hs, g, dens32, state, out, recv, fin, outbox,
                 dens_sem, hsend, hrecv, dsend, drecv, tsend, trecv, lsend, lrecv):
    cells, rows, cols = dens.shape
    nb, bands, halves = cols // CB, rows // RB, 2
    its = bands * halves
    zc = cells // its
    qrows = rows // nd
    width, rpp = outbox.shape[3], outbox.shape[2] // MOST
    groups = tsend.shape[0]
    me_d, me_t = lax.axis_index("depth"), lax.axis_index("tile")
    mesh_ids = pl.DeviceIdType.MESH

    barrier = pltpu.get_barrier_semaphore()

    @pl.loop(1, nt)
    def _(o):
        pl.semaphore_signal(barrier, inc=1, device_id=(me_d, lax.rem(me_t + o, nt)), device_id_type=mesh_ids)

    for k in range(1, nd):
        pl.semaphore_signal(barrier, inc=1, device_id=(lax.rem(me_d + k, nd), me_t), device_id_type=mesh_ids)

    def cols_of(b):
        return pl.ds(pl.multiple_of(b * CB, CB), CB)

    def pads_of(b):
        return pl.ds(pl.multiple_of(b * CB + PAD, PAD), CB)

    def dens_copy(b):
        return pltpu.make_async_copy(
            dens.at[:, :, cols_of(b)], d.at[pl.ds(1, cells), :, pads_of(b)], dens_sem.at[b])

    def halo(kind, b):
        src, dst, step = (
            (dens.at[cells - 1, :, cols_of(b)], d.at[0, :, pads_of(b)], 1),
            (dens.at[0, :, cols_of(b)], d.at[cells + 1, :, pads_of(b)], nd - 1),
            (ysend.at[0, :, cols_of(b)], hb.at[0, :, cols_of(b)], 1),
            (ysend.at[1, :, cols_of(b)], hb.at[1, :, cols_of(b)], nt - 1),
        )[kind]
        to = (lax.rem(me_d + step, nd), me_t) if kind < 2 else (me_d, lax.rem(me_t + step, nt))
        return pltpu.make_async_remote_copy(
            src_ref=src, dst_ref=dst, send_sem=hsend.at[kind, b], recv_sem=hrecv.at[kind, b],
            device_id=to, device_id_type=mesh_ids)

    sends = (me_d < nd - 1, me_d > 0, me_t < nt - 1, me_t > 0)
    gets = (me_d > 0, me_d < nd - 1, me_t > 0, me_t < nt - 1)

    @pl.loop(0, nb)
    def _(b):
        dens_copy(b).start()

    side = jnp.zeros((cells + 2, rows, PAD), d.dtype)
    d[:, :, :PAD] = side
    d[:, :, cols + PAD:] = side

    @pl.when(me_d == 0)
    def _():
        d[0, :, PAD:cols + PAD] = jnp.zeros((rows, cols), d.dtype)

    @pl.when(me_d == nd - 1)
    def _():
        d[cells + 1, :, PAD:cols + PAD] = jnp.zeros((rows, cols), d.dtype)

    @pl.when(me_t == 0)
    def _():
        hb[0] = jnp.zeros((cells, cols), hb.dtype)

    @pl.when(me_t == nt - 1)
    def _():
        hb[1] = jnp.zeros((cells, cols), hb.dtype)

    pl.semaphore_wait(barrier, nt - 1 + nd - 1)

    for kind in range(4):
        @pl.when(sends[kind])
        def _():
            @pl.loop(0, nb)
            def _(b):
                halo(kind, b).start()

    def label_copy(o):
        return pltpu.make_async_remote_copy(
            src_ref=labels.at[o], dst_ref=arrived.at[o], send_sem=lsend.at[o], recv_sem=lrecv.at[o],
            device_id=(me_d, lax.rem(me_t + o, nt)), device_id_type=mesh_ids)

    own_labels = pltpu.make_async_copy(labels.at[0], arrived.at[0], lsend.at[0])
    own_labels.start()

    @pl.loop(1, nt)
    def _(o):
        label_copy(o).start()

    def arrive(b):
        dens_copy(b).wait()
        for kind in range(4):
            @pl.when(gets[kind])
            def _():
                halo(kind, b).wait_recv()

    def spread(b):
        hs[...] = hb[:, :, cols_of(b)].astype(jnp.float32)

    ascend = rank[0] == 0
    facing = make_facing(d, g, dens32, hs, left, right, cells, rows, zc)

    def depth_copy(k, b, src):
        to = lax.rem(me_d + k, nd)
        return pltpu.make_async_remote_copy(
            src_ref=out.at[:, pl.ds(pl.multiple_of(to * qrows, 8), qrows), cols_of(b)],
            dst_ref=recv.at[src, :, :, cols_of(b)],
            send_sem=dsend.at[b, k], recv_sem=drecv.at[b, src],
            device_id=(to, me_t), device_id_type=mesh_ids)

    def depth_send(b):
        for k in range(1, nd):
            depth_copy(k, b, me_d).start()
        mine = out[:, pl.ds(pl.multiple_of(me_d * qrows, 8), qrows), cols_of(b)]
        recv[me_d, :, :, cols_of(b)] = mine

    def composite(b):
        for k in range(1, nd):
            depth_copy(k, b, lax.rem(me_d + k, nd)).wait_recv()
        color = recv[0, 0:3, :, cols_of(b)]
        trans = recv[0, 3, :, cols_of(b)]
        for i in range(1, nd):
            new = recv[i, 0:3, :, cols_of(b)]
            new_trans = recv[i, 3, :, cols_of(b)]
            front, back = jnp.where(ascend, color, new), jnp.where(ascend, new, color)
            color = front + jnp.where(ascend, trans, new_trans)[None] * back
            trans = trans * new_trans
        for ch in range(3):
            fin[ch, :, cols_of(b)] = color[ch] + trans * BACKDROP[ch]

    def tile_copy(o, part, window):
        return pltpu.make_async_remote_copy(
            src_ref=outbox.at[o, :, :, window], dst_ref=inbox.at[o, :, :, window],
            send_sem=tsend.at[part, o], recv_sem=trecv.at[part, o],
            device_id=(me_d, lax.rem(me_t + o, nt)), device_id_type=mesh_ids)

    def tile_own(part, window):
        return pltpu.make_async_copy(
            outbox.at[0, :, :, window], inbox.at[0, :, :, window], tsend.at[part, 0])

    def ship(part, window):
        @pl.loop(0, nt)
        def _(o):
            for m in range(MOST):
                p = route[o * MOST + m]
                for r in range(rpp):
                    if width == cols:
                        piece = fin[:, pl.ds(p * rpp + r, 1), window]
                    else:
                        per = cols // width
                        c = pl.multiple_of(lax.rem(p, per) * width, width)
                        piece = fin[:, pl.ds(lax.div(p, per), 1), pl.ds(c, width)]
                    outbox[o, :, m * rpp + r:m * rpp + r + 1, window] = piece

        tile_own(part, window).start()

        @pl.loop(1, nt)
        def _(o):
            tile_copy(o, part, window).start()

    arrive(0)
    arrive(1)
    spread(0)

    @pl.loop(0, its)
    def _(it):
        facing(0, 0, it)

    def finish(b):
        composite(b)
        if groups == nb:
            ship(b, cols_of(b))

    @pl.loop(0, nb)
    def _(b):
        @pl.when(b + 2 < nb)
        def _():
            arrive(b + 2)

        slot = lax.rem(b, 2)
        ahead = lax.rem(b + 1, nb)
        spread(ahead)

        @pl.loop(0, its)
        def _(it):
            facing(ahead, 1 - slot, it)
            rb = lax.div(it, halves)
            vals = march(dens32, g, state, ascend, slot, rb, lax.rem(it, halves), halves, cells)
            for ch, val in enumerate(vals):
                out[ch, pl.ds(pl.multiple_of(rb * RB, RB), RB), cols_of(b)] = val

        depth_send(b)

        @pl.when(b > 0)
        def _():
            finish(b - 1)

    finish(nb - 1)
    if groups != nb:
        ship(0, pl.ds(0, width))

    own_labels.wait()

    @pl.loop(1, nt)
    def _(o):
        label_copy(o).wait()

    @pl.loop(0, groups)
    def _(part):
        window = cols_of(part) if groups == nb else pl.ds(0, width)
        tile_own(part, window).wait()

        @pl.loop(1, nt)
        def _(o):
            tile_copy(o, part, window).wait()

    @pl.loop(0, nb)
    def _(b):
        for k in range(1, nd):
            depth_copy(k, b, me_d).wait_send()

    for kind in range(4):
        @pl.when(sends[kind])
        def _():
            @pl.loop(0, nb)
            def _(b):
                halo(kind, b).wait_send()


def place_kernel(arrived, inbox, display):
    nt, rpp, width = inbox.shape[0], inbox.shape[2] // MOST, inbox.shape[3]

    @pl.loop(0, nt)
    def _(o):
        for m in range(MOST):
            label = arrived[o, 0, m]

            @pl.when(label >= 0)
            def _():
                for r in range(rpp):
                    piece = inbox[o, :, m * rpp + r:m * rpp + r + 1, :]
                    display[:, 0, pl.ds(label, 1), r * width:(r + 1) * width] = piece


def on_device(density, depth_rank, piece_home):
    cells, rows, cols = density.shape
    nd, nt = lax.axis_size("depth"), lax.axis_size("tile")
    ppd = piece_home.shape[0]
    qrows = rows // nd
    piece_len = qrows * cols // ppd
    width = min(piece_len, cols)
    rpp = piece_len // width
    nb = cols // CB
    groups = nb if width == cols else 1

    order = jnp.arange(ppd, dtype=jnp.int32)
    owners = piece_home // ppd
    shared = (owners[:, None] == owners[None, :]) & (order[None, :] < order[:, None])
    earlier = jnp.sum(shared.astype(jnp.int32), axis=1)
    target = ((owners - lax.axis_index("tile") + nt) % nt) * MOST + earlier
    hit = jnp.arange(nt * MOST, dtype=jnp.int32)[:, None] == target[None, :]
    route = jnp.sum(jnp.where(hit, order[None, :], 0), axis=1)
    label = jnp.sum(jnp.where(hit, piece_home[None, :] % ppd + 1, 0), axis=1) - 1
    labels = jnp.pad(label.reshape(nt, 1, MOST), ((0, 0), (0, 0), (0, 128 - MOST)))

    ysend = jnp.stack([density[:, rows - 1], density[:, 0]])
    left, right = stencils(rows)
    anyspec = pl.BlockSpec(memory_space=pl.ANY)
    vmem = pl.BlockSpec(memory_space=pltpu.VMEM)
    smem = pl.BlockSpec(memory_space=pltpu.SMEM)
    dma = pltpu.SemaphoreType.DMA
    f32 = jnp.float32
    inbox, arrived = pl.pallas_call(
        lambda *refs: brick_kernel(nd, nt, *refs),
        out_shape=(jax.ShapeDtypeStruct((nt, 3, MOST * rpp, width), f32),
                   jax.ShapeDtypeStruct((nt, 1, 128), jnp.int32)),
        in_specs=[smem, smem, anyspec, anyspec, anyspec, vmem, vmem],
        out_specs=(anyspec, anyspec),
        scratch_shapes=[
            pltpu.VMEM((cells + 2, rows, cols + 2 * PAD), jnp.bfloat16),
            pltpu.VMEM((2, cells, cols), jnp.bfloat16),
            pltpu.VMEM((2, cells, CB), f32),
            pltpu.VMEM((2, cells, rows, CB), f32),
            pltpu.VMEM((2, cells, rows, CB), f32),
            pltpu.VMEM((5, RB, CB), f32),
            pltpu.VMEM((4, rows, cols), f32),
            pltpu.VMEM((nd, 4, qrows, cols), f32),
            pltpu.VMEM((3, qrows, cols), f32),
            pltpu.VMEM((nt, 3, MOST * rpp, width), f32),
            dma((nb,)), dma((4, nb)), dma((4, nb)), dma((nb, nd)), dma((nb, nd)),
            dma((groups, nt)), dma((groups, nt)), dma((nt,)), dma((nt,)),
        ],
        compiler_params=pltpu.CompilerParams(
            collective_id=0, has_side_effects=True, vmem_limit_bytes=56 * 1024 * 1024),
    )(depth_rank, route, density, ysend, labels, left, right)
    return pl.pallas_call(
        place_kernel,
        out_shape=jax.ShapeDtypeStruct((3, 1, ppd, piece_len), f32),
        in_specs=[smem, vmem],
        out_specs=vmem,
    )(arrived, inbox)


def solution(mesh):
    in_specs = (P("depth", "tile", None), P(), P("tile"))
    out_specs = P(None, "depth", "tile", None)
    return jax.shard_map(
        on_device, mesh=mesh, in_specs=in_specs, out_specs=out_specs, check_vma=False
    )
```

```python
import math
import jax
import jax.numpy as jnp
import numpy as np
from jax import lax
from jax.experimental import pallas as pl
from jax.experimental.pallas import tpu as pltpu
from jax.sharding import PartitionSpec as P

MOST = 2
EMPTY = -(2**30)

EXTINCT = 0.5
LIGHT_Z = 0.6
LIGHT_Y = 0.48
LIGHT_X = 0.64
SHARPNESS = 6.0
BACKDROP = (0.08, 0.1, 0.14)

PAD = 128
CB = 256
MC = 128
SIG_A = math.exp(-3.0)
SIG_B = math.exp(-2.5)
SIN = (0.9999999978529928,
       -0.1666666388441264,
       0.008333274854744043,
       -0.00019836767087186654,
       2.7400072109094996e-06,
       -2.2499595606831132e-08)


def inverse(x):
    return 1.0 / x


def stencils(rows):
    wy, wz = LIGHT_Y / LIGHT_X, LIGHT_Z / LIGHT_X
    left = np.zeros((rows, 3 * rows), np.float32)
    for r in range(rows):
        left[r, r] = -wz
        left[r, 2 * rows + r] = wz
        if r < rows - 1:
            left[r, rows + r + 1] = wy
        if r > 0:
            left[r, rows + r - 1] = -wy
    right = np.zeros((CB + 2 * PAD, CB), np.float32)
    for c in range(CB):
        right[c + PAD + 1, c] = 1.0
        right[c + PAD - 1, c] = -1.0
    return jnp.asarray(left, jnp.bfloat16), jnp.asarray(right, jnp.bfloat16)


def make_facing(d, g_pair, dens_pair, hs, left, right, cells, rows, zc):
    wy = LIGHT_Y / LIGHT_X

    def facing(block, slot, chunk):
        z0 = chunk * zc
        g, dens32 = g_pair[slot], dens_pair[slot]
        c0 = pl.multiple_of(block * CB, CB)
        wide = d[pl.ds(z0 + 1, zc), :, pl.ds(c0, CB + 2 * PAD)]
        dx = jnp.dot(wide.reshape(zc * rows, CB + 2 * PAD), right[...],
                     preferred_element_type=jnp.float32)
        c1 = pl.multiple_of(block * CB + PAD, PAD)
        sub = lax.broadcasted_iota(jnp.int32, (8, CB), 0)
        for i in range(zc):
            tall = d[pl.ds(z0 + i, 3), :, pl.ds(c1, CB)].reshape(3 * rows, CB)
            dyz = jnp.dot(left[...], tall, preferred_element_type=jnp.float32)
            both = dyz + dx[i * rows:(i + 1) * rows]
            low = hs[0, pl.ds(z0 + i, 1), :] * wy
            high = hs[1, pl.ds(z0 + i, 1), :] * wy
            g[z0 + i, 0:8] = both[0:8] - jnp.where(sub == 0, low, 0.0)
            g[z0 + i, 8:rows - 8] = both[8:rows - 8]
            g[z0 + i, rows - 8:rows] = both[rows - 8:] + jnp.where(sub == 7, high, 0.0)
            dens32[z0 + i] = wide[i, :, PAD:PAD + CB].astype(jnp.float32)

    return facing


def march(dens32, g, state, ascend, band, half, halves, cells, c0):
    steps = cells // halves
    first = half == 0
    lanes = slice(c0, c0 + MC)
    trans = jnp.where(first, 1.0, state[0, :, lanes])
    total, m0, m1, wave = (jnp.where(first, 0.0, state[i, :, lanes]) for i in range(1, 5))
    band_rows = state.shape[1]
    r0 = pl.multiple_of(band * band_rows, 8)
    bias = (0.35 + 0.65 * 0.5) / (0.65 * 0.5)
    for i in range(steps):
        k = half * steps + i
        z = jnp.where(ascend, k, cells - 1 - k)
        dens = dens32[z, pl.ds(r0, band_rows), lanes]
        face = g[z, pl.ds(r0, band_rows), lanes]
        shade = jnp.tanh(face * (0.5 * SHARPNESS * LIGHT_X)) + bias
        after = trans * jnp.exp2(dens * (-EXTINCT * math.log2(math.e)))
        ws = (trans - after) * shade
        trans = after
        u = dens + 0.01
        wr = ws * inverse((u + SIG_A) * (u + SIG_B))
        y = jnp.log(u) * (1.7 / 2) + math.pi / 2
        q = y * y
        c = SIN[-1]
        for coef in SIN[-2::-1]:
            c = c * q + coef
        c = c * y
        total = total + ws
        m0 = m0 + wr
        m1 = m1 + wr * u
        wave = wave + ws * (c * c)
    for i, val in enumerate((trans, total, m0, m1, wave)):
        state[i, :, lanes] = val
    scale = 0.65 * 0.5
    return (
        scale * (total - SIG_A * (m1 + SIG_B * m0)),
        scale * wave,
        scale * SIG_B * (m1 + SIG_A * m0),
        trans,
    )


def brick_kernel(nd, nt, pieces, rank, route, dens, ylast, yfirst, labels, left, right, inbox, arrived,
                 d, hb, hs, g0, g1, dens0, dens1, state, out, recv, fin, outbox,
                 dens_sem, hsend, hrecv, dsend, drecv, tsend, trecv, lsend, lrecv):
    cells, rows, cols = dens.shape
    nb, halves = cols // CB, 2
    its = nd * halves
    zc = cells // its
    qrows = rows // nd
    width, rpp = outbox.shape[3], outbox.shape[2] // MOST
    groups = tsend.shape[0]
    me_d, me_t = lax.axis_index("depth"), lax.axis_index("tile")
    mesh_ids = pl.DeviceIdType.MESH

    barrier = pltpu.get_barrier_semaphore()

    @pl.loop(1, nt)
    def _(o):
        pl.semaphore_signal(barrier, inc=1, device_id=(me_d, lax.rem(me_t + o, nt)), device_id_type=mesh_ids)

    for k in range(1, nd):
        pl.semaphore_signal(barrier, inc=1, device_id=(lax.rem(me_d + k, nd), me_t), device_id_type=mesh_ids)

    def cols_of(b):
        return pl.ds(pl.multiple_of(b * CB, CB), CB)

    def pads_of(b):
        return pl.ds(pl.multiple_of(b * CB + PAD, PAD), CB)

    def dens_copy(b):
        return pltpu.make_async_copy(
            dens.at[:, :, cols_of(b)], d.at[pl.ds(1, cells), :, pads_of(b)], dens_sem.at[b])

    def halo(kind, b):
        src, dst, step = (
            (dens.at[cells - 1, :, cols_of(b)], d.at[0, :, pads_of(b)], 1),
            (dens.at[0, :, cols_of(b)], d.at[cells + 1, :, pads_of(b)], nd - 1),
            (ylast.at[:, cols_of(b)], hb.at[0, :, cols_of(b)], 1),
            (yfirst.at[:, cols_of(b)], hb.at[1, :, cols_of(b)], nt - 1),
        )[kind]
        to = (lax.rem(me_d + step, nd), me_t) if kind < 2 else (me_d, lax.rem(me_t + step, nt))
        return pltpu.make_async_remote_copy(
            src_ref=src, dst_ref=dst, send_sem=hsend.at[kind, b], recv_sem=hrecv.at[kind, b],
            device_id=to, device_id_type=mesh_ids)

    sends = (me_d < nd - 1, me_d > 0, me_t < nt - 1, me_t > 0)
    gets = (me_d > 0, me_d < nd - 1, me_t > 0, me_t < nt - 1)

    @pl.loop(0, nb)
    def _(b):
        dens_copy(b).start()

    side = jnp.zeros((cells + 2, rows, PAD), d.dtype)
    d[:, :, :PAD] = side
    d[:, :, cols + PAD:] = side

    @pl.when(me_d == 0)
    def _():
        d[0, :, PAD:cols + PAD] = jnp.zeros((rows, cols), d.dtype)

    @pl.when(me_d == nd - 1)
    def _():
        d[cells + 1, :, PAD:cols + PAD] = jnp.zeros((rows, cols), d.dtype)

    @pl.when(me_t == 0)
    def _():
        hb[0] = jnp.zeros((cells, cols), hb.dtype)

    @pl.when(me_t == nt - 1)
    def _():
        hb[1] = jnp.zeros((cells, cols), hb.dtype)

    pl.semaphore_wait(barrier, nt - 1 + nd - 1)

    @pl.loop(0, nb)
    def _(b):
        for kind in range(4):
            @pl.when(sends[kind])
            def _():
                halo(kind, b).start()

    def label_copy(o):
        return pltpu.make_async_remote_copy(
            src_ref=labels.at[o], dst_ref=arrived.at[o], send_sem=lsend.at[o], recv_sem=lrecv.at[o],
            device_id=(me_d, lax.rem(me_t + o, nt)), device_id_type=mesh_ids)

    own_labels = pltpu.make_async_copy(labels.at[0], arrived.at[0], lsend.at[0])
    own_labels.start()

    @pl.loop(1, nt)
    def _(o):
        label_copy(o).start()

    def arrive(b):
        dens_copy(b).wait()
        for kind in range(4):
            @pl.when(gets[kind])
            def _():
                halo(kind, b).wait_recv()

    def spread(b):
        hs[...] = hb[:, :, cols_of(b)].astype(jnp.float32)

    ascend = rank[0] == 0
    g_pair, dens_pair = (g0, g1), (dens0, dens1)
    facing = make_facing(d, g_pair, dens_pair, hs, left, right, cells, rows, zc)

    def depth_copy(k, b, src):
        to = lax.rem(me_d + k, nd)
        return pltpu.make_async_remote_copy(
            src_ref=out.at[:, pl.ds(pl.multiple_of(to * qrows, 8), qrows), cols_of(b)],
            dst_ref=recv.at[src, :, :, cols_of(b)],
            send_sem=dsend.at[b, k], recv_sem=drecv.at[b, src],
            device_id=(to, me_t), device_id_type=mesh_ids)

    def keep_own(b):
        mine = out[:, pl.ds(pl.multiple_of(me_d * qrows, 8), qrows), cols_of(b)]
        recv[me_d, :, :, cols_of(b)] = mine

    def composite(b):
        for k in range(1, nd):
            depth_copy(k, b, lax.rem(me_d + k, nd)).wait_recv()
        color = recv[0, 0:3, :, cols_of(b)]
        trans = recv[0, 3, :, cols_of(b)]
        for i in range(1, nd):
            new = recv[i, 0:3, :, cols_of(b)]
            new_trans = recv[i, 3, :, cols_of(b)]
            front, back = jnp.where(ascend, color, new), jnp.where(ascend, new, color)
            color = front + jnp.where(ascend, trans, new_trans)[None] * back
            trans = trans * new_trans
        for ch in range(3):
            fin[ch, :, cols_of(b)] = color[ch] + trans * BACKDROP[ch]

    def tile_copy(o, part, window):
        return pltpu.make_async_remote_copy(
            src_ref=outbox.at[o, :, :, window], dst_ref=inbox.at[o, :, :, window],
            send_sem=tsend.at[part, o], recv_sem=trecv.at[part, o],
            device_id=(me_d, lax.rem(me_t + o, nt)), device_id_type=mesh_ids)

    def tile_own(part, window):
        return pltpu.make_async_copy(
            outbox.at[0, :, :, window], inbox.at[0, :, :, window], tsend.at[part, 0])

    def ship(part, window):
        @pl.loop(0, nt)
        def _(o):
            for m in range(MOST):
                p = lax.div((2 * m - 1) * route[o, 0, m], pieces)
                p = jnp.where(route[o, 0, m] == EMPTY, 0, p)
                for r in range(rpp):
                    if width == cols:
                        piece = fin[:, pl.ds(p * rpp + r, 1), window]
                    else:
                        per = cols // width
                        c = pl.multiple_of(lax.rem(p, per) * width, width)
                        piece = fin[:, pl.ds(lax.div(p, per), 1), pl.ds(c, width)]
                    outbox[o, :, m * rpp + r:m * rpp + r + 1, window] = piece

        tile_own(part, window).start()

        @pl.loop(1, nt)
        def _(o):
            tile_copy(o, part, window).start()

    arrive(0)
    arrive(1)
    spread(0)

    @pl.loop(0, its)
    def _(it):
        facing(0, 0, it)

    def finish(b):
        composite(b)
        if groups == nb:
            ship(b, cols_of(b))

    def step(b, slot):
        @pl.when(b + 2 < nb)
        def _():
            arrive(b + 2)

        ahead = lax.rem(b + 1, nb)
        spread(ahead)

        @pl.loop(0, its)
        def _(it):
            facing(ahead, 1 - slot, it)
            k = lax.div(it, halves) + 1
            half = lax.rem(it, halves)
            band = lax.rem(me_d + k, nd)
            for c0 in range(0, CB, MC):
                vals = march(dens_pair[slot], g_pair[slot], state, ascend, band, half, halves, cells, c0)
                lanes = pl.ds(pl.multiple_of(b * CB + c0, MC), MC)
                for ch, val in enumerate(vals):
                    out[ch, pl.ds(pl.multiple_of(band * qrows, 8), qrows), lanes] = val

            @pl.when((half == halves - 1) & (k < nd))
            def _():
                depth_copy(k, b, me_d).start()

        keep_own(b)

        @pl.when(b > 0)
        def _():
            finish(b - 1)

    @pl.loop(0, nb // 2)
    def _(pair):
        step(2 * pair, 0)
        step(2 * pair + 1, 1)

    finish(nb - 1)
    if groups != nb:
        ship(0, pl.ds(0, width))

    own_labels.wait()

    @pl.loop(1, nt)
    def _(o):
        label_copy(o).wait()

    @pl.loop(0, groups)
    def _(part):
        window = cols_of(part) if groups == nb else pl.ds(0, width)
        tile_own(part, window).wait()

        @pl.loop(1, nt)
        def _(o):
            tile_copy(o, part, window).wait()

    @pl.loop(0, nb)
    def _(b):
        for k in range(1, nd):
            depth_copy(k, b, me_d).wait_send()

    for kind in range(4):
        @pl.when(sends[kind])
        def _():
            @pl.loop(0, nb)
            def _(b):
                halo(kind, b).wait_send()


def place_kernel(arrived, inbox, display):
    nt, rpp, width = inbox.shape[0], inbox.shape[2] // MOST, inbox.shape[3]

    @pl.loop(0, nt)
    def _(o):
        for m in range(MOST):
            value = (2 * m - 1) * arrived[o, 0, m]
            label = lax.rem(value, display.shape[2])
            here = arrived[o, 0, m] != EMPTY
            if m:
                here = here & (value != -arrived[o, 0, 0])

            @pl.when(here)
            def _():
                for r in range(rpp):
                    piece = inbox[o, :, m * rpp + r:m * rpp + r + 1, :]
                    display[:, 0, pl.ds(label, 1), r * width:(r + 1) * width] = piece


def on_device(density, depth_rank, piece_home):
    cells, rows, cols = density.shape
    nd, nt = lax.axis_size("depth"), lax.axis_size("tile")
    ppd = piece_home.shape[0]
    qrows = rows // nd
    piece_len = qrows * cols // ppd
    width = min(piece_len, cols)
    rpp = piece_len // width
    nb = cols // CB
    groups = nb if width == cols else 1

    order = jnp.arange(ppd, dtype=jnp.int32)
    owners = piece_home // ppd
    code = order * ppd + piece_home % ppd
    offset = (owners - lax.axis_index("tile") + nt) % nt
    signs = jnp.where(jnp.arange(128) == 0, -1, 1)[None, None, :, None]
    goes = offset[None, None, None, :] == jnp.arange(nt)[:, None, None, None]
    codes = jnp.max(jnp.where(goes, signs * code[None, None, None, :], EMPTY), axis=3)
    ylast, yfirst = density[:, rows - 1], density[:, 0]
    left, right = stencils(rows)
    anyspec = pl.BlockSpec(memory_space=pl.ANY)
    vmem = pl.BlockSpec(memory_space=pltpu.VMEM)
    smem = pl.BlockSpec(memory_space=pltpu.SMEM)
    dma = pltpu.SemaphoreType.DMA
    f32 = jnp.float32
    inbox, arrived = pl.pallas_call(
        lambda *refs: brick_kernel(nd, nt, ppd, *refs),
        out_shape=(jax.ShapeDtypeStruct((nt, 3, MOST * rpp, width), f32),
                   jax.ShapeDtypeStruct((nt, 1, 128), jnp.int32)),
        in_specs=[smem, smem] + [anyspec] * 4 + [vmem] * 2,
        out_specs=(anyspec, anyspec),
        scratch_shapes=[
            pltpu.VMEM((cells + 2, rows, cols + 2 * PAD), jnp.bfloat16),
            pltpu.VMEM((2, cells, cols), jnp.bfloat16),
            pltpu.VMEM((2, cells, CB), f32),
            pltpu.VMEM((cells, rows, CB), f32),
            pltpu.VMEM((cells, rows, CB), f32),
            pltpu.VMEM((cells, rows, CB), f32),
            pltpu.VMEM((cells, rows, CB), f32),
            pltpu.VMEM((5, qrows, CB), f32),
            pltpu.VMEM((4, rows, cols), f32),
            pltpu.VMEM((nd, 4, qrows, cols), f32),
            pltpu.VMEM((3, qrows, cols), f32),
            pltpu.VMEM((nt, 3, MOST * rpp, width), f32),
            dma((nb,)), dma((4, nb)), dma((4, nb)), dma((nb, nd)), dma((nb, nd)),
            dma((groups, nt)), dma((groups, nt)), dma((nt,)), dma((nt,)),
        ],
        compiler_params=pltpu.CompilerParams(
            collective_id=0, has_side_effects=True, vmem_limit_bytes=56 * 1024 * 1024),
    )(depth_rank, codes, density, ylast, yfirst, codes, left, right)
    return pl.pallas_call(
        place_kernel,
        out_shape=jax.ShapeDtypeStruct((3, 1, ppd, piece_len), f32),
        in_specs=[smem, vmem],
        out_specs=vmem,
    )(arrived, inbox)


def solution(mesh):
    in_specs = (P("depth", "tile", None), P(), P("tile"))
    out_specs = P(None, "depth", "tile", None)
    return jax.shard_map(
        on_device, mesh=mesh, in_specs=in_specs, out_specs=out_specs, check_vma=False
    )
```
